32 devices in a mesh: cell: 2 (over x), row: 8 (over z, y), col: 2 (over core).
Axes of the slice: x: 2, y: 2, z: 4, core: 2. Of those that a mesh axis runs over, the one named last changes fastest.
Arguments:
- half_system: bfloat16 [32768, 32768], P(('cell', 'row'), 'col'), parts along dimension 0, may hold values from -6 to 6
- vectors: bfloat16 [65536, 512], P(('cell', 'col', 'row')), parts along dimension 0, may hold values from -0.03125 to 0.03125
- edge: bfloat16 [512, 64, 512], P(('cell', 'row'), None, 'col'), parts along dimension 0, may hold values from -6 to 6
- ket: bfloat16 [128, 128], P('cell'), parts along dimension 0, may hold values from -0.5 to 0.5
- bra: bfloat16 [128, 128], P('cell'), parts along dimension 0, may hold values from -0.75 to 0.75
Outputs:
- new_edge: bfloat16 [1024, 64, 512], P(('cell', 'row'), None, 'col'), parts along dimension 0
The draws below stay inside these ranges and needn't reach their ends.
There are 2 independent parts, one for each index of `cell`. The reference program is written for one: setup_inputs(seed, part) draws one part's arguments, and reference() takes and returns one part's arrays. A program takes and returns all parts, laid end to end along the dimension named above; each array names one. Nothing has to cross between parts.
All inputs are finite; a program needn't handle non-finite values.
Results may differ from the reference program's by a relative error of at most 0.0076.
Values may be sent and summed in bfloat16 or wider, within the bound.
A program may use at most 128 MiB of HBM per device.

```python
import jax
import jax.numpy as jnp

CHI = 512
D2 = 64
CL = 256
LEGS = 128
K = 32768
KR = 16384


def shard_levels(own_key, dims, shards, low, largest):
    level, own = 1.0, jax.random.fold_in(own_key, 6)
    for axis_at, parts in shards:
        heights = jnp.exp(jax.random.uniform(jax.random.fold_in(own, axis_at), (parts,), jnp.float32, low / len(shards), largest / len(shards)))
        level = level * jnp.repeat(heights, dims[axis_at] // parts).reshape([-1 if axis == axis_at else 1 for axis in range(len(dims))])
    return level


def noise(key, shape, spread, reach, cuts=(), kind=jnp.bfloat16):
    values = jax.random.normal(key, shape, jnp.float32) * spread
    if len(cuts) > 0:
        values = shard_levels(key, shape, cuts, -0.22, 0.18) * values
    return jnp.clip(values, min=-reach, max=reach).astype(kind)


def setup_inputs(seed: int = 0, part: int = 0) -> dict:
    streams_of = jax.random.split(jax.random.key(seed), 6)
    part_keys = jax.random.split(jax.random.fold_in(streams_of[5], part), 6)
    half_system = noise(part_keys[0], (KR, K), 1.0, 6.0, ((0, 8), (1, 2)))
    vectors = noise(part_keys[1], (K, CHI), K ** -0.5, 0.03125, ((0, 16),))
    edge = noise(part_keys[2], (CL, D2, CHI), 1.0, 6.0, ((0, 8), (2, 2)))
    ket = noise(part_keys[3], (D2, LEGS), LEGS ** -0.5, 0.5)
    bra = noise(part_keys[4], (D2, LEGS), D2 ** -0.5, 0.75)
    return {"half_system": half_system, "vectors": vectors, "edge": edge, "ket": ket, "bra": bra}


def reference(half_system, vectors, edge, ket, bra):
    projector = jnp.dot(half_system, vectors, preferred_element_type=jnp.float32).astype(jnp.bfloat16)
    layer = jnp.dot(ket, bra.T, preferred_element_type=jnp.float32).astype(jnp.bfloat16)
    absorbed = jnp.einsum('aub,us->asb', edge.astype(jnp.float32), layer.astype(jnp.float32)).astype(jnp.bfloat16)
    proj3 = projector.reshape(CL, D2, CHI)
    middle = jnp.einsum('asc,asb->scb', proj3.astype(jnp.float32), absorbed.astype(jnp.float32))
    middle = (middle * (CL ** -0.5)).astype(jnp.bfloat16)
    new_edge = jnp.einsum('ts,scb->ctb', layer.astype(jnp.float32), middle.astype(jnp.float32))
    return new_edge.astype(jnp.bfloat16)
```

```python
import functools

import jax
import jax.numpy as jnp
from jax import lax
from jax.experimental import pallas as pl
from jax.experimental.pallas import tpu as pltpu
from jax.sharding import PartitionSpec as P

MESH = pl.DeviceIdType.MESH
SUBS = 2
GROUP = 2


def plain(half_system, vectors, edge, ket, bra):
    partial_value = jnp.dot(
        half_system,
        lax.all_gather(vectors, "row", axis=0, tiled=True),
        preferred_element_type=jnp.float32,
    )
    projector = lax.psum_scatter(partial_value, "col", scatter_dimension=1, tiled=True).astype(
        jnp.bfloat16
    )
    layer = jnp.dot(ket, bra.T, preferred_element_type=jnp.float32).astype(jnp.bfloat16)
    absorbed = jnp.einsum("aub,us->asb", edge, layer, preferred_element_type=jnp.float32).astype(
        jnp.bfloat16
    )
    left_count, d2 = edge.shape[0], edge.shape[1]
    proj3 = projector.reshape(left_count, d2, projector.shape[1])
    moved_proj, moved_edge = (
        lax.all_to_all(proj3, "row", split_axis=1, concat_axis=0, tiled=True),
        lax.all_to_all(absorbed, "row", split_axis=1, concat_axis=0, tiled=True),
    )
    moved_proj = lax.all_gather(moved_proj, "col", axis=2, tiled=True)
    middle = jnp.einsum("asc,asb->scb", moved_proj, moved_edge, preferred_element_type=jnp.float32)
    middle = (middle * moved_edge.shape[0] ** (-0.5)).astype(jnp.bfloat16)
    regrouped = lax.all_to_all(middle, "row", split_axis=1, concat_axis=0, tiled=True)
    new_edge = jnp.einsum("ts,scb->ctb", layer, regrouped, preferred_element_type=jnp.float32)
    return new_edge.astype(jnp.bfloat16)


def row_at(place, rows):
    half = rows // 2
    return jnp.where(place < half, place * 2, (rows - 1 - place) * 2 + 1)


def kernel(
    n, left, sblk, cblk, scale,
    half_ref, vec_ref, abs_ref, out_ref,
    vbuf, hbuf, acc, xbuf, psend, gbuf, abuf, msend,
    lsem, hsem, vsend, vrecv, asend, arecv, xsem, psem_s, psem_r, msem_s, msem_r,
):
    row, col = lax.axis_index("row"), lax.axis_index("col")
    other = 1 - col
    place = jnp.where(lax.rem(row, 2) == 0, row // 2, n - 1 - row // 2)
    ahead = row_at(lax.rem(place + 1, n), n)
    behind = row_at(lax.rem(place + n - 1, n), n)
    kb = vec_ref.shape[0]
    piece = kb // (2 * SUBS)
    per = 2 * SUBS
    d2 = n * sblk
    hrows = half_ref.shape[0]
    tile = min(512, hrows)

    barrier = pltpu.get_barrier_semaphore()
    for step in range(1, n):
        peer = lax.rem(row + step, n)
        for c in range(2):
            pl.semaphore_signal(barrier, inc=1, device_id={"row": peer, "col": c}, device_id_type=MESH)
    pl.semaphore_signal(barrier, inc=1, device_id={"col": other}, device_id_type=MESH)

    def own(d, sub):
        start = (d * SUBS + sub) * piece
        return pltpu.make_async_copy(vec_ref.at[pl.ds(start, piece), :], vbuf.at[row, d, sub], lsem.at[d, sub])

    for sub in range(SUBS):
        for d in range(2):
            own(d, sub).start()

    def owner(s, d):
        return row_at(lax.rem(place - s + n, n) if d == 0 else lax.rem(place + s, n), n)

    def hcopy(s, k):
        sub, d = k // 2, k % 2
        start = pl.multiple_of(owner(s, d) * kb + (d * SUBS + sub) * piece, piece)
        return pltpu.make_async_copy(half_ref.at[:, pl.ds(start, piece)], hbuf.at[k], hsem.at[k])

    for k in range(per):
        hcopy(0, k).start()
    acc[...] = jnp.zeros_like(acc)

    def vcopy(s, sub, d):
        slot = vbuf.at[owner(s, d), d, sub]
        return pltpu.make_async_remote_copy(
            src_ref=slot, dst_ref=slot, send_sem=vsend.at[d, s, sub], recv_sem=vrecv.at[d, s, sub],
            device_id={"row": ahead if d == 0 else behind}, device_id_type=MESH,
        )

    def varrival(s, sub, d):
        slot = vbuf.at[owner(s + 1, d), d, sub]
        return pltpu.make_async_remote_copy(
            src_ref=slot, dst_ref=slot, send_sem=vsend.at[d, s, sub], recv_sem=vrecv.at[d, s, sub],
            device_id={"row": ahead if d == 0 else behind}, device_id_type=MESH,
        )

    def acopy(step, source):
        peer = lax.rem(row + step, n)
        where = row if source else lax.rem(row + n - step, n)
        dst = abuf.at[col, :, pl.ds(pl.multiple_of(where * left, left), left), :]
        return pltpu.make_async_remote_copy(
            src_ref=abs_ref.at[peer], dst_ref=dst, send_sem=asend.at[step], recv_sem=arecv.at[step],
            device_id={"row": peer}, device_id_type=MESH,
        )

    def aown():
        dst = abuf.at[col, :, pl.ds(pl.multiple_of(row * left, left), left), :]
        return pltpu.make_async_copy(abs_ref.at[row], dst, arecv.at[0])

    def apair(which):
        return pltpu.make_async_remote_copy(
            src_ref=abuf.at[which], dst_ref=abuf.at[which], send_sem=asend.at[n], recv_sem=arecv.at[n],
            device_id={"col": other}, device_id_type=MESH,
        )

    for sub in range(SUBS):
        for d in range(2):
            own(d, sub).wait()
    pl.semaphore_wait(barrier, 2 * (n - 1) + 1)

    @pl.loop(0, n)
    def _(s):
        for sub in range(SUBS):
            for d in range(2):
                @pl.when(s > 0)
                def _():
                    varrival(s - 1, sub, d).wait_recv()

                @pl.when(s < n - 1)
                def _():
                    vcopy(s, sub, d).start()

            if sub == SUBS - 1:
                @pl.when(s == 0)
                def _():
                    aown().start()
                    for step in range(1, n):
                        acopy(step, True).start()

                @pl.when(s == n // 2)
                def _():
                    aown().wait()
                    for step in range(1, n):
                        acopy(step, False).wait_recv()
                    apair(col).start()

            for d in range(2):
                k = 2 * sub + d
                hcopy(s, k).wait()

                @pl.loop(0, hrows // tile)
                def _(i):
                    rows = pl.ds(pl.multiple_of(i * tile, tile), tile)
                    value = jnp.dot(
                        hbuf[k, rows, :], vbuf[owner(s, d), d, sub], preferred_element_type=jnp.float32
                    )
                    for lane in range(acc.shape[0]):
                        acc[lane, rows, :] += value[:, lane * 128:(lane + 1) * 128]

                @pl.when(s < n - 1)
                def _():
                    hcopy(s + 1, k).start()

    lanes = acc.shape[0] // 2
    pair = pltpu.make_async_remote_copy(
        src_ref=acc.at[pl.ds(other * lanes, lanes)], dst_ref=xbuf, send_sem=xsem.at[0], recv_sem=xsem.at[1],
        device_id={"col": other}, device_id_type=MESH,
    )
    pair.start()
    pair.wait_recv()

    def pcopy(step, source):
        peer = lax.rem(row + step, n)
        where = row if source else lax.rem(row + n - step, n)
        dst = gbuf.at[:, pl.ds(pl.multiple_of(where * left, left), left), :]
        return pltpu.make_async_remote_copy(
            src_ref=psend.at[peer], dst_ref=dst, send_sem=psem_s.at[step], recv_sem=psem_r.at[step],
            device_id={"row": peer}, device_id_type=MESH,
        )

    def pown():
        dst = gbuf.at[:, pl.ds(pl.multiple_of(row * left, left), left), :]
        return pltpu.make_async_copy(psend.at[row], dst, psem_r.at[0])

    for step in list(range(1, n)) + [0]:
        peer = lax.rem(row + step, n)

        @pl.loop(0, sblk)
        def _(j):
            rows = pl.ds(peer * sblk + j, left, stride=d2)
            for lane in range(lanes):
                value = acc[col * lanes + lane, rows, :] + xbuf[lane, rows, :]
                psend[peer, j, :, lane * 128:(lane + 1) * 128] = value.astype(jnp.bfloat16)

        if step > 0:
            pcopy(step, True).start()
        else:
            pown().start()

    pown().wait()
    for step in range(1, n):
        pcopy(step, False).wait_recv()
    apair(other).wait_recv()

    rows_half = n // 2

    def mcopy(g, j, h):
        return pltpu.make_async_remote_copy(
            src_ref=msend.at[h, pl.ds(g * GROUP, GROUP), pl.ds(j * cblk, cblk), :],
            dst_ref=out_ref.at[pl.ds(row * sblk + g * GROUP, GROUP), :, :],
            send_sem=msem_s.at[g, j, h], recv_sem=msem_r.at[g, row],
            device_id={"row": col * rows_half + j, "col": h}, device_id_type=MESH,
        )

    def mown(g, j, h):
        return pltpu.make_async_copy(
            msend.at[h, pl.ds(g * GROUP, GROUP), pl.ds(j * cblk, cblk), :],
            out_ref.at[pl.ds(row * sblk + g * GROUP, GROUP), :, :],
            msem_s.at[g, j, h],
        )

    def is_self(j, h):
        return jnp.logical_and(col * rows_half + j == row, col == h)

    groups = sblk // GROUP
    for g in range(groups):
        for e in range(GROUP):
            at = g * GROUP + e
            for h in range(2):
                value = lax.dot_general(
                    gbuf[at], abuf[h, at], (((0,), (0,)), ((), ())), preferred_element_type=jnp.float32
                )
                msend[h, at] = (value * scale).astype(jnp.bfloat16)
        for j in range(rows_half):
            for h in range(2):
                same = is_self(j, h)

                @pl.when(same)
                def _():
                    mown(g, j, h).start()

                @pl.when(jnp.logical_not(same))
                def _():
                    mcopy(g, j, h).start()

    from_col = row // rows_half
    for g in range(groups):
        for q in range(n):
            @pl.when(jnp.logical_not(jnp.logical_and(row == q, from_col == col)))
            def _():
                dst = out_ref.at[pl.ds(q * sblk + g * GROUP, GROUP), :, :]
                pltpu.make_async_remote_copy(
                    src_ref=dst, dst_ref=dst, send_sem=msem_s.at[g, 0, 0], recv_sem=msem_r.at[g, q],
                    device_id={"col": other}, device_id_type=MESH,
                ).wait_recv()
        for j in range(rows_half):
            for h in range(2):
                same = is_self(j, h)

                @pl.when(same)
                def _():
                    mown(g, j, h).wait()

                @pl.when(jnp.logical_not(same))
                def _():
                    mcopy(g, j, h).wait_send()

    @pl.loop(0, n - 1)
    def _(s):
        for sub in range(SUBS):
            for d in range(2):
                vcopy(s, sub, d).wait_send()

    for step in range(1, n):
        acopy(step, True).wait_send()
        pcopy(step, True).wait_send()
    apair(col).wait_send()
    pair.wait_send()


def per_device(half_system, vectors, edge, ket, bra):
    n = lax.axis_size("row")
    left, d2, right = edge.shape
    kb, width = vectors.shape
    sblk, cblk = d2 // n, width // n
    fits = (
        lax.axis_size("col") == 2 and n % 2 == 0 and d2 % n == 0 and width % n == 0
        and left % 16 == 0 and cblk % 16 == 0 and sblk % GROUP == 0 and kb % (256 * SUBS) == 0
        and width % 256 == 0 and right % 128 == 0
    )
    if not fits:
        return plain(half_system, vectors, edge, ket, bra)
    bf16, f32 = jnp.bfloat16, jnp.float32
    layer = jnp.dot(ket, bra.T, preferred_element_type=f32).astype(bf16)
    absorbed = jnp.einsum("aub,us->sab", edge, layer, preferred_element_type=f32).astype(bf16)
    absorbed = absorbed.reshape(n, sblk, left, right)
    hrows, cols = half_system.shape
    piece = kb // (2 * SUBS)
    half = width // 2
    lanes = half // 128
    any_space = pl.BlockSpec(memory_space=pl.ANY)
    dma = pltpu.SemaphoreType.DMA
    regrouped = pl.pallas_call(
        functools.partial(kernel, n, left, sblk, cblk, float((n * left) ** -0.5)),
        out_shape=jax.ShapeDtypeStruct((d2, cblk, right), bf16),
        in_specs=[any_space] * 3,
        out_specs=any_space,
        scratch_shapes=[
            pltpu.VMEM((n, 2, SUBS, piece, width), bf16),
            pltpu.VMEM((2 * SUBS, hrows, piece), bf16),
            pltpu.VMEM((2 * lanes, hrows, 128), f32),
            pltpu.VMEM((lanes, hrows, 128), f32),
            pltpu.VMEM((n, sblk, left, half), bf16),
            pltpu.VMEM((sblk, n * left, half), bf16),
            pltpu.VMEM((2, sblk, n * left, right), bf16),
            pltpu.VMEM((2, sblk, half, right), bf16),
            dma((2, SUBS)),
            dma((2 * SUBS,)),
            dma((2, n - 1, SUBS)),
            dma((2, n - 1, SUBS)),
            dma((n + 1,)),
            dma((n + 1,)),
            dma((2,)),
            dma((n,)),
            dma((n,)),
            dma((sblk // GROUP, n // 2, 2)),
            dma((sblk // GROUP, n)),
        ],
        compiler_params=pltpu.CompilerParams(
            collective_id=0, has_side_effects=True, vmem_limit_bytes=60 * 1024 * 1024
        ),
        name="renormalize",
    )(half_system, vectors, absorbed)
    new_edge = jnp.einsum("ts,scb->ctb", layer, regrouped, preferred_element_type=f32)
    return new_edge.astype(bf16)


def solution(mesh):
    placed = (
        P(("cell", "row"), "col"),
        P(("cell", "col", "row"), None),
        P(("cell", "row"), None, "col"),
        P("cell", None),
        P("cell", None),
    )
    return jax.shard_map(
        per_device,
        mesh=mesh,
        in_specs=placed,
        out_specs=P(("cell", "row"), None, "col"),
        check_vma=False,
    )
```

```python
import functools

import jax
import jax.numpy as jnp
from jax import lax
from jax.experimental import pallas as pl
from jax.experimental.pallas import tpu as pltpu
from jax.sharding import PartitionSpec as P

MESH = pl.DeviceIdType.MESH
CHUNKS = 2
GROUP = 4


def plain(half_system, vectors, edge, ket, bra):
    partial_value = jnp.dot(
        half_system,
        lax.all_gather(vectors, "row", axis=0, tiled=True),
        preferred_element_type=jnp.float32,
    )
    projector = lax.psum_scatter(partial_value, "col", scatter_dimension=1, tiled=True).astype(
        jnp.bfloat16
    )
    layer = jnp.dot(ket, bra.T, preferred_element_type=jnp.float32).astype(jnp.bfloat16)
    absorbed = jnp.einsum("aub,us->asb", edge, layer, preferred_element_type=jnp.float32).astype(
        jnp.bfloat16
    )
    left_count, d2 = edge.shape[0], edge.shape[1]
    proj3 = projector.reshape(left_count, d2, projector.shape[1])
    moved_proj, moved_edge = (
        lax.all_to_all(proj3, "row", split_axis=1, concat_axis=0, tiled=True),
        lax.all_to_all(absorbed, "row", split_axis=1, concat_axis=0, tiled=True),
    )
    moved_proj = lax.all_gather(moved_proj, "col", axis=2, tiled=True)
    middle = jnp.einsum("asc,asb->scb", moved_proj, moved_edge, preferred_element_type=jnp.float32)
    middle = (middle * moved_edge.shape[0] ** (-0.5)).astype(jnp.bfloat16)
    regrouped = lax.all_to_all(middle, "row", split_axis=1, concat_axis=0, tiled=True)
    new_edge = jnp.einsum("ts,scb->ctb", layer, regrouped, preferred_element_type=jnp.float32)
    return new_edge.astype(jnp.bfloat16)


def kernel(
    n, left, sblk, cblk, scale,
    half_ref, vec_ref, abs_ref, out_ref,
    vbuf, hbuf, acc, xbuf, psend, gbuf, abuf, msend,
    lsem, hsem, vsend, vrecv, asend, arecv, xsem_s, xsem_r, psem_s, psem_r, msem_s, msem_r,
):
    row, col = lax.axis_index("row"), lax.axis_index("col")
    other = 1 - col
    z, y = row // 2, lax.rem(row, 2)
    far = n // 2
    kb = vec_ref.shape[0]
    ka = kb * 13 // 16
    d2 = n * sblk
    hrows = half_ref.shape[0]
    tile = min(256, hrows)
    visits = CHUNKS * far

    def zat(i):
        found = 0
        for zz in range(far):
            for at, value in enumerate(sorted(range(far), key=lambda w: abs(w - zz))):
                found = found + jnp.where(jnp.logical_and(z == zz, i == at), value, 0)
        return found

    barrier = pltpu.get_barrier_semaphore()
    for step in range(1, n):
        peer = lax.rem(row + step, n)
        for c in range(2):
            pl.semaphore_signal(barrier, inc=1, device_id={"row": peer, "col": c}, device_id_type=MESH)
    pl.semaphore_signal(barrier, inc=1, device_id={"col": other}, device_id_type=MESH)

    def lane_of(q, c):
        return 3 * c if q == 0 else 1 + c

    def own(q, c):
        return pltpu.make_async_copy(
            vec_ref.at[:, pl.ds(lane_of(q, c) * 128, 128)],
            vbuf.at[q, row, :, pl.ds(c * 128, 128)],
            lsem.at[q, c],
        )

    for q in range(CHUNKS):
        for c in range(2):
            own(q, c).start()

    def hcopy(v, yy, k):
        start = pl.multiple_of((zat(lax.rem(v, far)) * 2 + yy) * kb, kb)
        return pltpu.make_async_copy(half_ref.at[:, pl.ds(start, kb)], hbuf.at[k], hsem.at[k])

    hcopy(0, y, 0).start()
    hcopy(0, 1 - y, 1).start()
    acc[...] = jnp.zeros_like(acc)

    def vcopy(q, zi, yy, part, way):
        r = zi * 2 + yy
        slot = vbuf.at[q, r, pl.ds(0, ka) if part == 0 else pl.ds(ka, kb - ka), :]
        peer = (z + 1) * 2 + y if way == 0 else (z - 1) * 2 + y if way == 1 else z * 2 + 1 - y
        return pltpu.make_async_remote_copy(
            src_ref=slot, dst_ref=slot, send_sem=vsend.at[q, r, part, way], recv_sem=vrecv.at[q, r, part],
            device_id={"row": peer}, device_id_type=MESH,
        )

    def each_way(zi, mine, part, first, do):
        @pl.when(jnp.logical_and(zi <= z, z < far - 1))
        def _():
            do(0)

        @pl.when(jnp.logical_and(zi >= z, z > 0))
        def _():
            do(1)

        if mine and part == 0:
            do(2)
        if mine and part == 1:
            @pl.when(first)
            def _():
                do(2)

    def acopy(step, source):
        peer = lax.rem(row + step, n)
        where = row if source else lax.rem(row + n - step, n)
        dst = abuf.at[col, :, pl.ds(pl.multiple_of(where * left, left), left), :]
        return pltpu.make_async_remote_copy(
            src_ref=abs_ref.at[peer], dst_ref=dst, send_sem=asend.at[step], recv_sem=arecv.at[step],
            device_id={"row": peer}, device_id_type=MESH,
        )

    def aown():
        dst = abuf.at[col, :, pl.ds(pl.multiple_of(row * left, left), left), :]
        return pltpu.make_async_copy(abs_ref.at[row], dst, arecv.at[0])

    def apair(which):
        return pltpu.make_async_remote_copy(
            src_ref=abuf.at[which], dst_ref=abuf.at[which], send_sem=asend.at[n], recv_sem=arecv.at[n],
            device_id={"col": other}, device_id_type=MESH,
        )

    def multiply(v, yy, k):
        q = v // far
        r = zat(lax.rem(v, far)) * 2 + yy
        hcopy(v, yy, k).wait()

        @pl.loop(0, hrows // tile)
        def _(i):
            rows = pl.ds(pl.multiple_of(i * tile, tile), tile)
            value = jnp.dot(hbuf[k, rows, :], vbuf[q, r], preferred_element_type=jnp.float32)
            for lane in range(2):
                acc[q, lane, rows, :] += value[:, lane * 128:(lane + 1) * 128]

    def pair(q):
        return pltpu.make_async_remote_copy(
            src_ref=acc.at[q, other], dst_ref=xbuf.at[q], send_sem=xsem_s.at[q], recv_sem=xsem_r.at[q],
            device_id={"col": other}, device_id_type=MESH,
        )

    def pcopy(q, step, source):
        peer = lax.rem(row + step, n)
        where = row if source else lax.rem(row + n - step, n)
        dst = gbuf.at[q, :, pl.ds(pl.multiple_of(where * left, left), left), :]
        return pltpu.make_async_remote_copy(
            src_ref=psend.at[q, peer], dst_ref=dst, send_sem=psem_s.at[q, step], recv_sem=psem_r.at[q, step],
            device_id={"row": peer}, device_id_type=MESH,
        )

    def pown(q):
        dst = gbuf.at[q, :, pl.ds(pl.multiple_of(row * left, left), left), :]
        return pltpu.make_async_copy(psend.at[q, row], dst, psem_r.at[q, 0])

    def project(q):
        pair(q).start()
        pair(q).wait_recv()
        mine = acc.at[q, col]
        theirs = xbuf.at[q]

        @pl.loop(0, n)
        def _(at):
            peer = lax.rem(row + 1 + at, n)

            @pl.loop(0, sblk)
            def _(j):
                rows = pl.ds(peer * sblk + j, left, stride=d2)
                psend[q, peer, j] = (mine[rows, :] + theirs[rows, :]).astype(jnp.bfloat16)

        for step in range(1, n):
            pcopy(q, step, True).start()
        pown(q).start()

    def mcopy(q, g, j, h):
        return pltpu.make_async_remote_copy(
            src_ref=msend.at[q, h, pl.ds(g * GROUP, GROUP), pl.ds(j * cblk, cblk), :],
            dst_ref=out_ref.at[pl.ds(row * sblk + g * GROUP, GROUP), :, :],
            send_sem=msem_s.at[q, g, j, h], recv_sem=msem_r.at[g, row],
            device_id={"row": lane_of(q, col) * 2 + j, "col": h}, device_id_type=MESH,
        )

    def mown(q, g, j, h):
        return pltpu.make_async_copy(
            msend.at[q, h, pl.ds(g * GROUP, GROUP), pl.ds(j * cblk, cblk), :],
            out_ref.at[pl.ds(row * sblk + g * GROUP, GROUP), :, :],
            msem_s.at[q, g, j, h],
        )

    groups = sblk // GROUP

    def every(q, g, local, remote):
        for j in range(2):
            for h in range(2):
                same = jnp.logical_and(lane_of(q, col) * 2 + j == row, col == h)

                @pl.when(same)
                def _():
                    local(mown(q, g, j, h))

                @pl.when(jnp.logical_not(same))
                def _():
                    remote(mcopy(q, g, j, h))

    def renormalize(q):
        pown(q).wait()
        for step in range(1, n):
            pcopy(q, step, False).wait_recv()
        if q == 0:
            apair(other).wait_recv()
        for g in range(groups):
            for e in range(GROUP):
                at = g * GROUP + e
                for h in range(2):
                    value = lax.dot_general(
                        gbuf[q, at], abuf[h, at], (((0,), (0,)), ((), ())),
                        preferred_element_type=jnp.float32,
                    )
                    msend[q, h, at] = (value * scale).astype(jnp.bfloat16)
            every(q, g, lambda copy: copy.start(), lambda copy: copy.start())

    for q in range(CHUNKS):
        for c in range(2):
            own(q, c).wait()
    pl.semaphore_wait(barrier, 2 * (n - 1) + 1)

    def take(v, mine, part):
        q, i = v // far, lax.rem(v, far)
        zi = zat(i)
        yy = y if mine else 1 - y

        def wait():
            vcopy(q, zi, yy, part, 2).wait_recv()

        if mine:
            pl.when(i > 0)(wait)
        else:
            wait()
        if mine or part == 1:
            each_way(zi, mine, part, i == 0, lambda way: vcopy(q, zi, yy, part, way).start())

    @pl.loop(0, visits)
    def _(v):
        take(v, True, 0)
        take(v, True, 1)

        @pl.when(v == 0)
        def _():
            aown().start()
            for step in range(1, n):
                acopy(step, True).start()

        multiply(v, y, 0)

        @pl.when(v < visits - 1)
        def _():
            hcopy(v + 1, y, 0).start()

        take(v, False, 1)

        @pl.when(v > 0)
        def _():
            take(v - 1, False, 0)
            multiply(v - 1, 1 - y, 1)
            hcopy(v, 1 - y, 1).start()

        @pl.when(v == 2)
        def _():
            aown().wait()
            for step in range(1, n):
                acopy(step, False).wait_recv()
            apair(col).start()

        @pl.when(v == far)
        def _():
            project(0)

        @pl.when(v == far + 1)
        def _():
            renormalize(0)

    take(visits - 1, False, 0)
    multiply(visits - 1, 1 - y, 1)
    project(1)
    renormalize(1)

    from_col = row // (n // 2)
    for g in range(groups):
        for w in range(n):
            @pl.when(jnp.logical_not(jnp.logical_and(row == w, from_col == col)))
            def _():
                dst = out_ref.at[pl.ds(w * sblk + g * GROUP, GROUP), :, :]
                pltpu.make_async_remote_copy(
                    src_ref=dst, dst_ref=dst, send_sem=msem_s.at[0, g, 0, 0], recv_sem=msem_r.at[g, w],
                    device_id={"col": other}, device_id_type=MESH,
                ).wait_recv()
        for q in range(CHUNKS):
            every(q, g, lambda copy: copy.wait(), lambda copy: copy.wait_send())

    @pl.loop(0, visits)
    def _(v):
        q, i = v // far, lax.rem(v, far)
        zi = zat(i)
        for mine, part in ((True, 0), (True, 1), (False, 1)):
            yy = y if mine else 1 - y
            each_way(zi, mine, part, i == 0, lambda way: vcopy(q, zi, yy, part, way).wait_send())

    for step in range(1, n):
        acopy(step, True).wait_send()
        for q in range(CHUNKS):
            pcopy(q, step, True).wait_send()
    apair(col).wait_send()
    for q in range(CHUNKS):
        pair(q).wait_send()


def per_device(half_system, vectors, edge, ket, bra):
    n = lax.axis_size("row")
    left, d2, right = edge.shape
    kb, width = vectors.shape
    sblk, cblk = d2 // n, width // n
    fits = (
        lax.axis_size("col") == 2 and n == 8 and d2 % n == 0 and width == 512
        and left % 16 == 0 and sblk % GROUP == 0 and kb % 256 == 0 and right % 128 == 0
    )
    if not fits:
        return plain(half_system, vectors, edge, ket, bra)
    bf16, f32 = jnp.bfloat16, jnp.float32
    layer = jnp.dot(ket, bra.T, preferred_element_type=f32).astype(bf16)
    absorbed = jnp.einsum("aub,us->sab", edge, layer, preferred_element_type=f32).astype(bf16)
    absorbed = absorbed.reshape(n, sblk, left, right)
    hrows, cols = half_system.shape
    half = width // 4
    any_space = pl.BlockSpec(memory_space=pl.ANY)
    dma = pltpu.SemaphoreType.DMA
    regrouped = pl.pallas_call(
        functools.partial(kernel, n, left, sblk, cblk, float((n * left) ** -0.5)),
        out_shape=jax.ShapeDtypeStruct((d2, cblk, right), bf16),
        in_specs=[any_space] * 3,
        out_specs=any_space,
        scratch_shapes=[
            pltpu.VMEM((CHUNKS, n, kb, 2 * half), bf16),
            pltpu.VMEM((2, hrows, kb), bf16),
            pltpu.VMEM((CHUNKS, 2, hrows, half), f32),
            pltpu.VMEM((CHUNKS, hrows, half), f32),
            pltpu.VMEM((CHUNKS, n, sblk, left, half), bf16),
            pltpu.VMEM((CHUNKS, sblk, n * left, half), bf16),
            pltpu.VMEM((2, sblk, n * left, right), bf16),
            pltpu.VMEM((CHUNKS, 2, sblk, half, right), bf16),
            dma((CHUNKS, 2)),
            dma((2,)),
            dma((CHUNKS, n, 2, 3)),
            dma((CHUNKS, n, 2)),
            dma((n + 1,)),
            dma((n + 1,)),
            dma((CHUNKS,)),
            dma((CHUNKS,)),
            dma((CHUNKS, n)),
            dma((CHUNKS, n)),
            dma((CHUNKS, sblk // GROUP, 2, 2)),
            dma((sblk // GROUP, n)),
        ],
        compiler_params=pltpu.CompilerParams(
            collective_id=0, has_side_effects=True, vmem_limit_bytes=60 * 1024 * 1024
        ),
        name="renormalize",
    )(half_system, vectors, absorbed)
    new_edge = jnp.einsum("ts,scb->ctb", layer, regrouped, preferred_element_type=f32)
    return new_edge.astype(bf16)


def solution(mesh):
    placed = (
        P(("cell", "row"), "col"),
        P(("cell", "col", "row"), None),
        P(("cell", "row"), None, "col"),
        P("cell", None),
        P("cell", None),
    )
    return jax.shard_map(
        per_device,
        mesh=mesh,
        in_specs=placed,
        out_specs=P(("cell", "row"), None, "col"),
        check_vma=False,
    )
```

```python
import functools

import jax
import jax.numpy as jnp
from jax import lax
from jax.experimental import pallas as pl
from jax.experimental.pallas import tpu as pltpu
from jax.sharding import PartitionSpec as P

MESH = pl.DeviceIdType.MESH
SUBS = 2
GROUP = 4


def plain(half_system, vectors, edge, ket, bra):
    partial_value = jnp.dot(
        half_system,
        lax.all_gather(vectors, "row", axis=0, tiled=True),
        preferred_element_type=jnp.float32,
    )
    projector = lax.psum_scatter(partial_value, "col", scatter_dimension=1, tiled=True).astype(
        jnp.bfloat16
    )
    layer = jnp.dot(ket, bra.T, preferred_element_type=jnp.float32).astype(jnp.bfloat16)
    absorbed = jnp.einsum("aub,us->asb", edge, layer, preferred_element_type=jnp.float32).astype(
        jnp.bfloat16
    )
    left_count, d2 = edge.shape[0], edge.shape[1]
    proj3 = projector.reshape(left_count, d2, projector.shape[1])
    moved_proj, moved_edge = (
        lax.all_to_all(proj3, "row", split_axis=1, concat_axis=0, tiled=True),
        lax.all_to_all(absorbed, "row", split_axis=1, concat_axis=0, tiled=True),
    )
    moved_proj = lax.all_gather(moved_proj, "col", axis=2, tiled=True)
    middle = jnp.einsum("asc,asb->scb", moved_proj, moved_edge, preferred_element_type=jnp.float32)
    middle = (middle * moved_edge.shape[0] ** (-0.5)).astype(jnp.bfloat16)
    regrouped = lax.all_to_all(middle, "row", split_axis=1, concat_axis=0, tiled=True)
    new_edge = jnp.einsum("ts,scb->ctb", layer, regrouped, preferred_element_type=jnp.float32)
    return new_edge.astype(jnp.bfloat16)


def row_at(place, rows):
    half = rows // 2
    return jnp.where(place < half, place * 2, (rows - 1 - place) * 2 + 1)


def kernel(
    n, left, sblk, cblk, scale,
    half_ref, vec_ref, abs_ref, out_ref,
    vbuf, hbuf, acc, xbuf, psend, gbuf, abuf, msend,
    lsem, hsem, vsend, vrecv, asend, arecv, xsem, psem_s, psem_r, msem_s, msem_r,
):
    row, col = lax.axis_index("row"), lax.axis_index("col")
    other = 1 - col
    place = jnp.where(lax.rem(row, 2) == 0, row // 2, n - 1 - row // 2)
    ahead = row_at(lax.rem(place + 1, n), n)
    behind = row_at(lax.rem(place + n - 1, n), n)
    kb = vec_ref.shape[0]
    piece = kb // (2 * SUBS)
    per = 2 * SUBS
    d2 = n * sblk
    hrows = half_ref.shape[0]
    tile = min(512, hrows)

    barrier = pltpu.get_barrier_semaphore()
    for step in range(1, n):
        peer = lax.rem(row + step, n)
        for c in range(2):
            pl.semaphore_signal(barrier, inc=1, device_id={"row": peer, "col": c}, device_id_type=MESH)
    pl.semaphore_signal(barrier, inc=1, device_id={"col": other}, device_id_type=MESH)

    def own(d, sub):
        start = (d * SUBS + sub) * piece
        return pltpu.make_async_copy(vec_ref.at[pl.ds(start, piece), :], vbuf.at[row, d, sub], lsem.at[d, sub])

    for sub in range(SUBS):
        for d in range(2):
            own(d, sub).start()

    def owner(s, d):
        return row_at(lax.rem(place - s + n, n) if d == 0 else lax.rem(place + s, n), n)

    def hcopy(s, k):
        sub, d = k // 2, k % 2
        start = pl.multiple_of(owner(s, d) * kb + (d * SUBS + sub) * piece, piece)
        return pltpu.make_async_copy(half_ref.at[:, pl.ds(start, piece)], hbuf.at[k], hsem.at[k])

    for k in range(per):
        hcopy(0, k).start()
    acc[...] = jnp.zeros_like(acc)

    def vcopy(s, sub, d):
        slot = vbuf.at[owner(s, d), d, sub]
        return pltpu.make_async_remote_copy(
            src_ref=slot, dst_ref=slot, send_sem=vsend.at[d, s, sub], recv_sem=vrecv.at[d, s, sub],
            device_id={"row": ahead if d == 0 else behind}, device_id_type=MESH,
        )

    def varrival(s, sub, d):
        slot = vbuf.at[owner(s + 1, d), d, sub]
        return pltpu.make_async_remote_copy(
            src_ref=slot, dst_ref=slot, send_sem=vsend.at[d, s, sub], recv_sem=vrecv.at[d, s, sub],
            device_id={"row": ahead if d == 0 else behind}, device_id_type=MESH,
        )

    def acopy(step, source):
        peer = lax.rem(row + step, n)
        where = row if source else lax.rem(row + n - step, n)
        dst = abuf.at[col, :, pl.ds(pl.multiple_of(where * left, left), left), :]
        return pltpu.make_async_remote_copy(
            src_ref=abs_ref.at[peer], dst_ref=dst, send_sem=asend.at[step], recv_sem=arecv.at[step],
            device_id={"row": peer}, device_id_type=MESH,
        )

    def aown():
        dst = abuf.at[col, :, pl.ds(pl.multiple_of(row * left, left), left), :]
        return pltpu.make_async_copy(abs_ref.at[row], dst, arecv.at[0])

    def apair(which):
        return pltpu.make_async_remote_copy(
            src_ref=abuf.at[which], dst_ref=abuf.at[which], send_sem=asend.at[n], recv_sem=arecv.at[n],
            device_id={"col": other}, device_id_type=MESH,
        )

    for sub in range(SUBS):
        for d in range(2):
            own(d, sub).wait()
    pl.semaphore_wait(barrier, 2 * (n - 1) + 1)

    @pl.loop(0, n)
    def _(s):
        for sub in range(SUBS):
            for d in range(2):
                @pl.when(s > 0)
                def _():
                    varrival(s - 1, sub, d).wait_recv()

                @pl.when(s < n - 1)
                def _():
                    vcopy(s, sub, d).start()

            if sub == SUBS - 1:
                @pl.when(s == 0)
                def _():
                    aown().start()
                    for step in range(1, n):
                        acopy(step, True).start()

                @pl.when(s == n // 2)
                def _():
                    aown().wait()
                    for step in range(1, n):
                        acopy(step, False).wait_recv()
                    apair(col).start()

            for d in range(2):
                k = 2 * sub + d
                hcopy(s, k).wait()

                @pl.loop(0, hrows // tile)
                def _(i):
                    rows = pl.ds(pl.multiple_of(i * tile, tile), tile)
                    value = jnp.dot(
                        hbuf[k, rows, :], vbuf[owner(s, d), d, sub], preferred_element_type=jnp.float32
                    )
                    for lane in range(acc.shape[0]):
                        acc[lane, rows, :] += value[:, lane * 128:(lane + 1) * 128]

                @pl.when(s < n - 1)
                def _():
                    hcopy(s + 1, k).start()

    lanes = acc.shape[0] // 2

    def pair(lane):
        return pltpu.make_async_remote_copy(
            src_ref=acc.at[other * lanes + lane], dst_ref=xbuf.at[lane],
            send_sem=xsem.at[0, lane], recv_sem=xsem.at[1, lane],
            device_id={"col": other}, device_id_type=MESH,
        )

    def pcopy(lane, step, source):
        peer = lax.rem(row + step, n)
        where = row if source else lax.rem(row + n - step, n)
        dst = gbuf.at[lane, :, pl.ds(pl.multiple_of(where * left, left), left), :]
        return pltpu.make_async_remote_copy(
            src_ref=psend.at[lane, peer], dst_ref=dst,
            send_sem=psem_s.at[lane, step], recv_sem=psem_r.at[lane, step],
            device_id={"row": peer}, device_id_type=MESH,
        )

    def pown(lane):
        dst = gbuf.at[lane, :, pl.ds(pl.multiple_of(row * left, left), left), :]
        return pltpu.make_async_copy(psend.at[lane, row], dst, psem_r.at[lane, 0])

    for lane in range(lanes):
        pair(lane).start()
    for lane in range(lanes):
        pair(lane).wait_recv()
        for step in list(range(1, n)) + [0]:
            peer = lax.rem(row + step, n)

            @pl.loop(0, sblk)
            def _(j):
                rows = pl.ds(peer * sblk + j, left, stride=d2)
                value = acc[col * lanes + lane, rows, :] + xbuf[lane, rows, :]
                psend[lane, peer, j] = value.astype(jnp.bfloat16)

            if step > 0:
                pcopy(lane, step, True).start()
            else:
                pown(lane).start()

    apair(other).wait_recv()

    rows_half = n // 2

    def mcopy(g, j, h):
        return pltpu.make_async_remote_copy(
            src_ref=msend.at[h, pl.ds(g * GROUP, GROUP), pl.ds(j * cblk, cblk), :],
            dst_ref=out_ref.at[pl.ds(row * sblk + g * GROUP, GROUP), :, :],
            send_sem=msem_s.at[g, j, h], recv_sem=msem_r.at[g, row],
            device_id={"row": col * rows_half + j, "col": h}, device_id_type=MESH,
        )

    def mown(g, j, h):
        return pltpu.make_async_copy(
            msend.at[h, pl.ds(g * GROUP, GROUP), pl.ds(j * cblk, cblk), :],
            out_ref.at[pl.ds(row * sblk + g * GROUP, GROUP), :, :],
            msem_s.at[g, j, h],
        )

    def is_self(j, h):
        return jnp.logical_and(col * rows_half + j == row, col == h)

    groups = sblk // GROUP
    each = 128 // cblk
    for lane in range(lanes):
        pown(lane).wait()
        for step in range(1, n):
            pcopy(lane, step, False).wait_recv()
        for g in range(groups):
            for e in range(GROUP):
                at = g * GROUP + e
                for h in range(2):
                    value = lax.dot_general(
                        gbuf[lane, at], abuf[h, at], (((0,), (0,)), ((), ())),
                        preferred_element_type=jnp.float32,
                    )
                    msend[h, at, lane * 128:(lane + 1) * 128, :] = (value * scale).astype(jnp.bfloat16)
            for j in range(lane * each, (lane + 1) * each):
                for h in range(2):
                    same = is_self(j, h)

                    @pl.when(same)
                    def _():
                        mown(g, j, h).start()

                    @pl.when(jnp.logical_not(same))
                    def _():
                        mcopy(g, j, h).start()

    from_col = row // rows_half
    for g in range(groups):
        for q in range(n):
            @pl.when(jnp.logical_not(jnp.logical_and(row == q, from_col == col)))
            def _():
                dst = out_ref.at[pl.ds(q * sblk + g * GROUP, GROUP), :, :]
                pltpu.make_async_remote_copy(
                    src_ref=dst, dst_ref=dst, send_sem=msem_s.at[g, 0, 0], recv_sem=msem_r.at[g, q],
                    device_id={"col": other}, device_id_type=MESH,
                ).wait_recv()
        for j in range(rows_half):
            for h in range(2):
                same = is_self(j, h)

                @pl.when(same)
                def _():
                    mown(g, j, h).wait()

                @pl.when(jnp.logical_not(same))
                def _():
                    mcopy(g, j, h).wait_send()

    @pl.loop(0, n - 1)
    def _(s):
        for sub in range(SUBS):
            for d in range(2):
                vcopy(s, sub, d).wait_send()

    for step in range(1, n):
        acopy(step, True).wait_send()
        for lane in range(lanes):
            pcopy(lane, step, True).wait_send()
    apair(col).wait_send()
    for lane in range(lanes):
        pair(lane).wait_send()


def per_device(half_system, vectors, edge, ket, bra):
    n = lax.axis_size("row")
    left, d2, right = edge.shape
    kb, width = vectors.shape
    sblk, cblk = d2 // n, width // n
    fits = (
        lax.axis_size("col") == 2 and n % 2 == 0 and d2 % n == 0 and width % n == 0
        and left % 16 == 0 and cblk % 16 == 0 and sblk % GROUP == 0 and kb % (256 * SUBS) == 0
        and width % 256 == 0 and 128 % cblk == 0 and right % 128 == 0
    )
    if not fits:
        return plain(half_system, vectors, edge, ket, bra)
    bf16, f32 = jnp.bfloat16, jnp.float32
    layer = jnp.dot(ket, bra.T, preferred_element_type=f32).astype(bf16)
    absorbed = jnp.einsum("aub,us->sab", edge, layer, preferred_element_type=f32).astype(bf16)
    absorbed = absorbed.reshape(n, sblk, left, right)
    hrows, cols = half_system.shape
    piece = kb // (2 * SUBS)
    half = width // 2
    lanes = half // 128
    any_space = pl.BlockSpec(memory_space=pl.ANY)
    dma = pltpu.SemaphoreType.DMA
    regrouped = pl.pallas_call(
        functools.partial(kernel, n, left, sblk, cblk, float((n * left) ** -0.5)),
        out_shape=jax.ShapeDtypeStruct((d2, cblk, right), bf16),
        in_specs=[any_space] * 3,
        out_specs=any_space,
        scratch_shapes=[
            pltpu.VMEM((n, 2, SUBS, piece, width), bf16),
            pltpu.VMEM((2 * SUBS, hrows, piece), bf16),
            pltpu.VMEM((2 * lanes, hrows, 128), f32),
            pltpu.VMEM((lanes, hrows, 128), f32),
            pltpu.VMEM((lanes, n, sblk, left, 128), bf16),
            pltpu.VMEM((lanes, sblk, n * left, 128), bf16),
            pltpu.VMEM((2, sblk, n * left, right), bf16),
            pltpu.VMEM((2, sblk, half, right), bf16),
            dma((2, SUBS)),
            dma((2 * SUBS,)),
            dma((2, n - 1, SUBS)),
            dma((2, n - 1, SUBS)),
            dma((n + 1,)),
            dma((n + 1,)),
            dma((2, lanes)),
            dma((lanes, n)),
            dma((lanes, n)),
            dma((sblk // GROUP, n // 2, 2)),
            dma((sblk // GROUP, n)),
        ],
        compiler_params=pltpu.CompilerParams(
            collective_id=0, has_side_effects=True, vmem_limit_bytes=60 * 1024 * 1024
        ),
        name="renormalize",
    )(half_system, vectors, absorbed)
    new_edge = jnp.einsum("ts,scb->ctb", layer, regrouped, preferred_element_type=f32)
    return new_edge.astype(bf16)


def solution(mesh):
    placed = (
        P(("cell", "row"), "col"),
        P(("cell", "col", "row"), None),
        P(("cell", "row"), None, "col"),
        P("cell", None),
        P("cell", None),
    )
    return jax.shard_map(
        per_device,
        mesh=mesh,
        in_specs=placed,
        out_specs=P(("cell", "row"), None, "col"),
        check_vma=False,
    )
```
